128 devices in a mesh: igrp: 8 (over x, core), jgrp: 16 (over y, z).
Axes of the slice: x: 4, y: 4, z: 4, core: 2. Of those that a mesh axis runs over, the one named last changes fastest.
Arguments:
- t_start: bfloat16 [64, 64, 256, 256], P('igrp', 'jgrp'), may hold values from -2.390625 to 2.390625
- integrals: bfloat16 [64, 64, 256, 256], P('igrp', 'jgrp'), may hold values from -6 to 6
- weights: bfloat16 [64, 8, 256, 256], P('igrp'), may hold values from -0.125 to 0.125
- neighbours: int32 [64, 8], replicated, may hold values from 0 to 63, as said below
- eps_occ: float32 [64], replicated, may hold values from -2 to -0.5
- eps_vir: float32 [256], replicated, may hold values from 0.2 to 4
Outputs:
- amplitudes: float32 [64, 64, 256, 256], P('igrp', 'jgrp')
The draws below stay inside these ranges and needn't reach their ends.
Inputs may be any that keep to these rules, and one draw needn't show every extreme that they name: `neighbours`: the entries of a row are distinct. For every block of 8 consecutive rows starting at a multiple of 8, and every block of 8 consecutive orbitals starting at a multiple of 8, exactly 2 distinct orbitals of that block appear in those rows.
All inputs are finite; a program needn't handle non-finite values.
Results may differ from the reference program's by a relative error of at most 0.0018.
Values may be sent and summed in bfloat16 or wider, within the bound.
A program may use at most 128 MiB of HBM per device.

```python
import math
import jax
import jax.numpy as jnp
from jax import lax

NOCC = 64
V = 256
NNB = 8
CAP = 2
ITERS = 2
OI_DEV = 8


def draw_neighbours(key, part):
    groups = NOCC // OI_DEV
    allowed = CAP * groups
    first_key, second_key = jax.random.split(jax.random.fold_in(key, 7))
    scores = jax.random.randint(first_key, (groups, groups, OI_DEV), 0, 2 ** 20)
    scores = scores * OI_DEV + jnp.arange(OI_DEV, dtype=jnp.int32)[None, None, :]
    chosen = jnp.argsort(scores, axis=2)[:, :, :CAP].astype(jnp.int32)
    listed = chosen + (jnp.arange(groups, dtype=jnp.int32) * OI_DEV)[None, :, None]
    listed = listed.reshape(groups, allowed)
    shuffle = jax.random.randint(second_key, (groups, allowed), 0, 2 ** 20)
    shuffle = shuffle * allowed + jnp.arange(allowed, dtype=jnp.int32)[None, :]
    ordering = jnp.argsort(shuffle, axis=1).astype(jnp.int32)
    position = (jnp.arange(OI_DEV, dtype=jnp.int32)[:, None] * NNB + jnp.arange(NNB, dtype=jnp.int32)[None, :]) % allowed

    def per_group(group_list, group_order):
        return group_list[group_order[position]]
    result = jax.vmap(per_group)(listed, ordering)
    return result.reshape(NOCC, NNB).astype(jnp.int32)


def shard_levels(own_key, dims, cuts, low, high):
    def one(dim, parts):
        steps = jax.random.uniform(jax.random.fold_in(jax.random.fold_in(own_key, 6), dim), (parts,), jnp.float32, low / len(cuts), high / len(cuts))
        return jnp.repeat(jnp.exp(steps), dims[dim] // parts).reshape((-1,) + (1,) * (len(dims) - dim - 1))

    level = one(*cuts[0])
    for cut in cuts[1:]:
        level = level * one(*cut)
    return level


def centred(rng, extent, deviation, reach, shards=(), kind=jnp.bfloat16):
    values = jax.random.normal(rng, extent, jnp.float32) * deviation
    if len(shards) > 0:
        values = shard_levels(rng, extent, shards, -0.22, 0.18) * values
    return jnp.clip(values, min=-reach, max=reach).astype(kind)


def setup_inputs(seed: int = 0) -> dict:
    seeds = jax.random.split(jax.random.key(seed), 7)
    t_start = centred(seeds[0], (NOCC, NOCC, V, V), 0.3, 2.390625, ((0, 8), (1, 16)))
    integrals = centred(seeds[1], (NOCC, NOCC, V, V), 1.0, 6.0, ((0, 8), (1, 16)))
    weights = centred(seeds[2], (NOCC, NNB, V, V), (NNB * V) ** -0.5, 0.125, ((0, 8),))
    neighbours = draw_neighbours(jax.random.fold_in(seeds[6], 71), 0)
    eps_occ = jnp.clip(jax.random.uniform(seeds[4], (NOCC,), jnp.float32, -2.0, -0.5), -2.0, -0.5)
    eps_vir = jnp.clip(jnp.exp(jax.random.uniform(seeds[5], (V,), jnp.float32, math.log(0.2), math.log(4.0))), 0.2, 4.0)
    return dict(t_start=t_start, integrals=integrals, weights=weights, neighbours=neighbours, eps_occ=eps_occ, eps_vir=eps_vir)


def cycle_product(current, weights, neighbours):
    def per_orbital(inputs):
        weight_rows, listed = inputs
        blocks = jnp.take(current, listed, axis=0)
        return jnp.einsum('mac,mjcb->jab', weight_rows.astype(jnp.float32), blocks.astype(jnp.float32))
    return lax.map(per_orbital, (weights, neighbours)).astype(jnp.bfloat16)


def reference(t_start, integrals, weights, neighbours, eps_occ, eps_vir):
    denominator = (eps_vir[None, None, :, None] + eps_vir[None, None, None, :]
                   - eps_occ[:, None, None, None] - eps_occ[None, :, None, None])
    current = t_start
    updated = t_start.astype(jnp.float32)
    for sweep in range(ITERS):
        cycle_term = cycle_product(current, weights, neighbours)
        flipped = cycle_term.transpose(1, 0, 3, 2)
        updated = (integrals.astype(jnp.float32) + cycle_term.astype(jnp.float32)
                   + flipped.astype(jnp.float32)) / denominator
        current = updated.astype(jnp.bfloat16)
    return updated
```

```python
import functools

import jax
import jax.numpy as jnp
from jax import lax
from jax.experimental import pallas as pl
from jax.experimental.pallas import tpu as pltpu
from jax.sharding import PartitionSpec as P

NNB = 8
CAP = 2
ITERS = 2
MESH = pl.DeviceIdType.MESH
NX, NC, NY, NZ = 4, 2, 4, 4
CHUNKS = 4
ROWS = 8
ORDER = ((2, 0), (1, 0), (3, 0), (2, 1), (1, 1), (3, 1), (0, 1))


def first_true(flags, capacity):
    counted = flags.shape[1]
    ranking = jnp.cumsum(flags.astype(jnp.int32), axis=1) - 1
    offsets = jnp.arange(counted, dtype=jnp.int32)
    hits = flags[:, :, None] & (
        ranking[:, :, None] == jnp.arange(capacity, dtype=jnp.int32)[None, None, :]
    )
    return jnp.sum(offsets[None, :, None] * hits.astype(jnp.int32), axis=1)


def sweep_kernel(
    choice, slot, occ_rows, occ_cols, vir, t_h, k_h, w_h, out_h,
    t_0, t_1, t_2, t_3, k_v, w_v, pk, r_0, r_1, r_2, r_3, cs, b1, b2, fl, eye, stage,
    load_sem, es, er, s1s, s1r, s2s, s2r, s3s, s3r, out_sem,
):
    ig = lax.axis_index("igrp")
    jg = lax.axis_index("jgrp")
    x, c = ig // NC, ig % NC
    y, z = jg // NZ, jg % NZ
    received = (r_0, r_1, r_2, r_3)
    t_v = (t_0, t_1, t_2, t_3)

    def peer(dx, dc):
        return lax.rem(x + dx, NX) * NC + lax.rem(c + dc, NC)

    t_load = [
        pltpu.make_async_copy(t_h.at[:, q], t_v[q], load_sem.at[q]) for q in range(CHUNKS)
    ]
    w_load = pltpu.make_async_copy(w_h, w_v, load_sem.at[CHUNKS])
    k_load = pltpu.make_async_copy(k_h, k_v, load_sem.at[CHUNKS + 1])
    for load in t_load:
        load.start()
    w_load.start()
    k_load.start()

    barrier = pltpu.get_barrier_semaphore()
    inside = z // 2 == c
    for dx, dc in ORDER:
        pl.semaphore_signal(barrier, inc=1, device_id=(peer(dx, dc), jg), device_id_type=MESH)
    for dy in range(1, NY):
        pl.semaphore_signal(
            barrier, inc=1, device_id=(ig, lax.rem(y + dy, NY) * NZ + z), device_id_type=MESH
        )
    for dy in range(NY):
        for h in range(2):
            def greet(dy=dy, h=h):
                pl.semaphore_signal(
                    barrier,
                    inc=1,
                    device_id=(x * NC + z // 2, lax.rem(y + dy, NY) * NZ + 2 * c + h),
                    device_id_type=MESH,
                )
            if dy == 0:
                pl.when(jnp.logical_not(inside & (z == 2 * c + h)))(greet)
            else:
                greet()

    def pack(q):
        t_load[q].wait()

        def one(n, carry):
            kk = n // CAP
            s = n % CAP
            dest = peer(kk // NC, kk % NC)
            pk[q, n] = t_v[q][choice[dest * CAP + s]]
            return carry

        lax.fori_loop(CAP, NX * NC * CAP, one, 0)
        for s in range(CAP):
            received[q][ig * CAP + s] = t_v[q][choice[ig * CAP + s]]

    def exchange(q):
        copies = []
        for dx, dc in ORDER:
            kk = dx * NC + dc
            copies.append(
                pltpu.make_async_remote_copy(
                    src_ref=pk.at[q, pl.ds(kk * CAP, CAP)],
                    dst_ref=received[q].at[pl.ds(ig * CAP, CAP)],
                    send_sem=es.at[q, kk],
                    recv_sem=er.at[q, kk],
                    device_id=(peer(dx, dc), jg),
                    device_id_type=MESH,
                )
            )
        return copies

    def first_stage(q, dy):
        to = lax.rem(y + dy, NY)
        return pltpu.make_async_remote_copy(
            src_ref=cs.at[q, to],
            dst_ref=b1.at[q, y],
            send_sem=s1s.at[q, dy],
            recv_sem=s1r.at[q, dy],
            device_id=(ig, to * NZ + z),
            device_id_type=MESH,
        )

    def second_stage(q, dx):
        to = lax.rem(x + dx, NX)
        return pltpu.make_async_remote_copy(
            src_ref=b1.at[q, to],
            dst_ref=b2.at[q, x],
            send_sem=s2s.at[q, dx],
            recv_sem=s2r.at[q, dx],
            device_id=(to * NC + c, jg),
            device_id_type=MESH,
        )

    def third_stage(q, dx, h):
        source = lax.rem(x + NX - dx, NX)
        own = inside & (source == y) & (z == 2 * c + h)

        def remote():
            return pltpu.make_async_remote_copy(
                src_ref=b2.at[q, source, h],
                dst_ref=fl.at[q, z % 2, y],
                send_sem=s3s.at[q, dx, h],
                recv_sem=s3r.at[q, z % 2, y],
                device_id=(x * NC + z // 2, source * NZ + 2 * c + h),
                device_id_type=MESH,
            )

        def local():
            return pltpu.make_async_copy(
                b2.at[q, source, h], fl.at[q, z % 2, y], s3r.at[q, z % 2, y]
            )

        return own, remote, local

    def forward(q):
        for dy in range(1, NY):
            first_stage(q, dy).wait_recv()
        b2[q, x] = b1[q, x]
        for dx in range(1, NX):
            second_stage(q, dx).start()

    def finish(q):
        for half in range(2):
            for col in range(4):
                block = fl.at[q, half, col]
                pltpu.make_async_copy(block, block, s3r.at[q, half, col]).wait()
        update(q)

    def compute(q):
        blocks = received[q]

        def per_row(i, carry):
            total = jnp.zeros((256, 256), jnp.float32)
            for m in range(NNB):
                total += jnp.dot(
                    w_v[i, m], blocks[slot[i * NNB + m]], preferred_element_type=jnp.float32
                )
            cs[q, i % 4, i // 4] = total.astype(jnp.bfloat16)
            return carry

        lax.fori_loop(0, ROWS, per_row, 0)

    def update(q):
        def per_pair(n, carry):
            half = n // 4
            col = n % 4
            row = 4 * half + q
            flipped = lax.dot_general(
                eye[...], fl[q, half, col], (((1,), (1,)), ((), ())),
                preferred_element_type=jnp.float32,
            )
            total = (
                k_v[row, col].astype(jnp.float32) + cs[col, q, half].astype(jnp.float32) + flipped
            )
            value = total / (vir[...] - occ_rows[row] - occ_cols[col])
            stage[q, half, col] = value.astype(stage.dtype)
            return carry

        lax.fori_loop(0, 8, per_pair, 0)
        for half in range(2):
            out_copy(q, half).start()

    def out_copy(q, half):
        return pltpu.make_async_copy(
            stage.at[q, half], out_h.at[4 * half + q], out_sem.at[q, half]
        )

    rows_of = lax.broadcasted_iota(jnp.int32, (256, 256), 0)
    cols_of = lax.broadcasted_iota(jnp.int32, (256, 256), 1)
    eye[...] = jnp.where(rows_of == cols_of, 1.0, 0.0).astype(jnp.bfloat16)
    pack(0)
    pl.semaphore_wait(barrier, 18 - inside.astype(jnp.int32))

    for q in range(CHUNKS):
        if q + 1 < CHUNKS:
            pack(q + 1)
        for copy in exchange(q):
            copy.start()

    w_load.wait()
    for q in range(CHUNKS):
        for copy in exchange(q):
            copy.wait_recv()
        compute(q)
        b1[q, y] = cs[q, y]
        for dy in range(1, NY):
            first_stage(q, dy).start()
        if q >= 1:
            forward(q - 1)
    forward(CHUNKS - 1)
    k_load.wait()
    for q in range(CHUNKS):
        for dx in range(NX):
            if dx > 0:
                second_stage(q, dx).wait_recv()
            for h in range(2):
                own, remote, local = third_stage(q, dx, h)
                pl.when(jnp.logical_not(own))(lambda remote=remote: remote().start())
                pl.when(own)(lambda local=local: local().start())
        if q >= 1:
            finish(q - 1)
    finish(CHUNKS - 1)

    for q in range(CHUNKS):
        for copy in exchange(q):
            copy.wait_send()
        for dy in range(1, NY):
            first_stage(q, dy).wait_send()
        for dx in range(1, NX):
            second_stage(q, dx).wait_send()
        for dx in range(NX):
            for h in range(2):
                own, remote, local = third_stage(q, dx, h)
                pl.when(jnp.logical_not(own))(lambda remote=remote: remote().wait_send())
        for half in range(2):
            out_copy(q, half).wait()


def sweep(call_id, dtype, choice, slot, occ_rows, occ_cols, vir, current, integrals, weights):
    block = (256, 256)
    bf16 = jnp.bfloat16
    smem = pl.BlockSpec(memory_space=pltpu.SMEM)
    anywhere = pl.BlockSpec(memory_space=pl.ANY)
    dma = pltpu.SemaphoreType.DMA
    return pl.pallas_call(
        sweep_kernel,
        out_shape=jax.ShapeDtypeStruct((ROWS, CHUNKS) + block, dtype),
        in_specs=[smem] * 4 + [pl.BlockSpec(memory_space=pltpu.VMEM)] + [anywhere] * 3,
        out_specs=anywhere,
        scratch_shapes=[pltpu.VMEM((ROWS,) + block, bf16)] * CHUNKS
        + [
            pltpu.VMEM((ROWS, CHUNKS) + block, bf16),
            pltpu.VMEM((ROWS, NNB) + block, bf16),
            pltpu.VMEM((CHUNKS, NX * NC * CAP) + block, bf16),
        ]
        + [pltpu.VMEM((NX * NC * CAP,) + block, bf16)] * CHUNKS
        + [pltpu.VMEM((CHUNKS, 4, 2) + block, bf16)] * 3
        + [
            pltpu.VMEM((CHUNKS, 2, 4) + block, bf16),
            pltpu.VMEM(block, bf16),
            pltpu.VMEM((CHUNKS, 2, 4) + block, dtype),
            dma((CHUNKS + 2,)),
            dma((CHUNKS, 8)),
            dma((CHUNKS, 8)),
            dma((CHUNKS, 4)),
            dma((CHUNKS, 4)),
            dma((CHUNKS, 4)),
            dma((CHUNKS, 4)),
            dma((CHUNKS, 4, 2)),
            dma((CHUNKS, 2, 4)),
            dma((CHUNKS, 2)),
        ],
        compiler_params=pltpu.CompilerParams(
            collective_id=call_id, has_side_effects=True, vmem_limit_bytes=67043328
        ),
        name=f"sweep_{call_id}",
    )(choice, slot, occ_rows, occ_cols, vir, current, integrals, weights)


def body(t_start, integrals, weights, neighbours, eps_occ, eps_vir):
    row_count = weights.shape[0]
    col_count = t_start.shape[1]
    capacity = CAP
    igroups = lax.axis_size("igrp")
    my_igrp = lax.axis_index("igrp")
    my_jgrp = lax.axis_index("jgrp")
    grouped = neighbours.reshape(igroups, row_count * NNB)
    own_orbitals = my_igrp * row_count + jnp.arange(row_count, dtype=jnp.int32)
    wanted = jnp.any(grouped[:, :, None] == own_orbitals[None, None, :], axis=1)
    send_choice = first_true(wanted, capacity).reshape(-1)
    my_rows = lax.dynamic_slice_in_dim(neighbours, my_igrp * row_count, row_count, 0)
    flat_list = my_rows.reshape(-1)
    all_blocks = jnp.arange(igroups * row_count, dtype=jnp.int32).reshape(igroups, row_count)
    needed = jnp.any(flat_list[None, None, :] == all_blocks[:, :, None], axis=2)
    recv_orbitals = (
        first_true(needed, capacity) + (jnp.arange(igroups, dtype=jnp.int32) * row_count)[:, None]
    ).reshape(-1)
    slot_index = jnp.sum(
        jnp.arange(igroups * capacity, dtype=jnp.int32)[None, None, :]
        * (my_rows[:, :, None] == recv_orbitals[None, None, :]).astype(jnp.int32),
        axis=2,
    ).reshape(-1)
    occ_rows = lax.dynamic_slice_in_dim(eps_occ, my_igrp * row_count, row_count, 0)
    occ_cols = lax.dynamic_slice_in_dim(eps_occ, my_jgrp * col_count, col_count, 0)
    vir = eps_vir[:, None] + eps_vir[None, :]
    current = t_start
    for step in range(ITERS):
        dtype = jnp.float32 if step == ITERS - 1 else jnp.bfloat16
        current = sweep(
            step, dtype, send_choice, slot_index, occ_rows, occ_cols, vir, current, integrals, weights
        )
    return current


def solution(mesh):
    placed = (
        P("igrp", "jgrp", None, None),
        P("igrp", "jgrp", None, None),
        P("igrp", None, None, None),
        P(),
        P(),
        P(),
    )
    return jax.shard_map(
        body, mesh=mesh, in_specs=placed, out_specs=P("igrp", "jgrp", None, None), check_vma=False
    )
```

```python
import functools

import jax
import jax.numpy as jnp
from jax import lax
from jax.experimental import pallas as pl
from jax.experimental.pallas import tpu as pltpu
from jax.sharding import PartitionSpec as P

NNB = 8
CAP = 2
ITERS = 2
MESH = pl.DeviceIdType.MESH
NX, NC, NY, NZ = 4, 2, 4, 4
CHUNKS = 4
ROWS = 8
ORDER = ((2, 0), (1, 0), (3, 0), (2, 1), (1, 1), (3, 1), (0, 1))


def sweeps_kernel(
    masks, listed, occ, eps, t_h, k_h, w_h, out_h,
    t_0, t_1, t_2, t_3, k_v, w_v, pk, r_0, r_1, r_2, r_3, cs, b1, b2, fl, eye, vir, stage,
    choice, slot, load_sem, es, er, s1s, s1r, s2s, s2r, s3s, s3r, out_sem, free,
):
    ig = lax.axis_index("igrp")
    jg = lax.axis_index("jgrp")
    x, c = ig // NC, ig % NC
    y, z = jg // NZ, jg % NZ
    received = (r_0, r_1, r_2, r_3)
    t_v = (t_0, t_1, t_2, t_3)

    def peer(dx, dc):
        return lax.rem(x + dx, NX) * NC + lax.rem(c + dc, NC)

    t_load = [
        pltpu.make_async_copy(t_h.at[:, q], t_v[q], load_sem.at[q]) for q in range(CHUNKS)
    ]
    w_load = pltpu.make_async_copy(w_h, w_v, load_sem.at[CHUNKS])
    k_load = pltpu.make_async_copy(k_h, k_v, load_sem.at[CHUNKS + 1])
    for load in t_load:
        load.start()

    barrier = pltpu.get_barrier_semaphore()
    inside = z // 2 == c
    for dx, dc in ORDER:
        pl.semaphore_signal(barrier, inc=1, device_id=(peer(dx, dc), jg), device_id_type=MESH)
    for dy in range(1, NY):
        pl.semaphore_signal(
            barrier, inc=1, device_id=(ig, lax.rem(y + dy, NY) * NZ + z), device_id_type=MESH
        )
    def meet(dy, h, sem):
        def greet():
            pl.semaphore_signal(
                sem,
                inc=1,
                device_id=(x * NC + z // 2, lax.rem(y + dy, NY) * NZ + 2 * c + h),
                device_id_type=MESH,
            )

        if dy == 0:
            pl.when(jnp.logical_not(inside & (z == 2 * c + h)))(greet)
        else:
            greet()

    for dy in range(NY):
        for h in range(2):
            meet(dy, h, barrier)

    def place(bit):
        found = jnp.int32(0)
        for k in range(1, ROWS):
            found += (bit >= (1 << k)).astype(jnp.int32)
        return found

    def choose(p, carry):
        mask = masks[p, ig]
        low = mask & (0 - mask)
        choice[p * CAP] = place(low)
        choice[p * CAP + 1] = place(mask - low)
        return carry

    def locate(n, carry):
        orbital = listed[n % NNB, ig * ROWS + n // NNB]
        block = orbital // ROWS
        below = masks[ig, block] % lax.shift_left(jnp.int32(1), orbital % ROWS)
        slot[n] = block * CAP + (below > 0).astype(jnp.int32)
        return carry

    def pack(q):
        def one(n, carry):
            kk = n // CAP
            s = n % CAP
            dest = peer(kk // NC, kk % NC)
            pk[q, n] = t_v[q][choice[dest * CAP + s]]
            return carry

        lax.fori_loop(CAP, NX * NC * CAP, one, 0)
        for s in range(CAP):
            received[q][ig * CAP + s] = t_v[q][choice[ig * CAP + s]]

    def exchange(q):
        copies = []
        for dx, dc in ORDER:
            kk = dx * NC + dc
            copies.append(
                pltpu.make_async_remote_copy(
                    src_ref=pk.at[q, pl.ds(kk * CAP, CAP)],
                    dst_ref=received[q].at[pl.ds(ig * CAP, CAP)],
                    send_sem=es.at[q, kk],
                    recv_sem=er.at[q, kk],
                    device_id=(peer(dx, dc), jg),
                    device_id_type=MESH,
                )
            )
        return copies

    def start(copies):
        own, remote, local = copies
        pl.when(jnp.logical_not(own))(lambda: remote().start())
        pl.when(own)(lambda: local().start())

    def sent(copies):
        own, remote, local = copies
        pl.when(jnp.logical_not(own))(lambda: remote().wait_send())

    def landed(block, sem):
        pltpu.make_async_copy(block, block, sem).wait()

    def first_stage(q, dy, h):
        to = lax.rem(y + dy, NY)
        own = inside & (z == 2 * c + h) if dy == 0 else None
        source, target, arrival = cs.at[q, to, h], b1.at[q, y, z % 2], s1r.at[q, y, z % 2]

        def remote():
            return pltpu.make_async_remote_copy(
                src_ref=source,
                dst_ref=target,
                send_sem=s1s.at[q, dy, h],
                recv_sem=arrival,
                device_id=(x * NC + z // 2, to * NZ + 2 * c + h),
                device_id_type=MESH,
            )

        return own, remote, lambda: pltpu.make_async_copy(source, target, arrival)

    def second_stage(q, dx):
        to = lax.rem(x + dx, NX)
        return pltpu.make_async_remote_copy(
            src_ref=b1.at[q, to],
            dst_ref=b2.at[q, x],
            send_sem=s2s.at[q, dx],
            recv_sem=s2r.at[q, dx],
            device_id=(to * NC + c, jg),
            device_id_type=MESH,
        )

    def third_stage(q, dx):
        to = lax.rem(x + NX - dx, NX)
        source, target, arrival = b2.at[q, to], fl.at[q, y], s3r.at[q, y]

        def remote():
            return pltpu.make_async_remote_copy(
                src_ref=source,
                dst_ref=target,
                send_sem=s3s.at[q, dx],
                recv_sem=arrival,
                device_id=(ig, to * NZ + z),
                device_id_type=MESH,
            )

        return to == y, remote, lambda: pltpu.make_async_copy(source, target, arrival)

    def settle(q):
        for dy in range(NY):
            for h in range(2):
                copies = first_stage(q, dy, h)
                if dy == 0:
                    sent(copies)
                else:
                    copies[1]().wait_send()
        for dx in range(1, NX):
            second_stage(q, dx).wait_send()
        for dx in range(NX):
            sent(third_stage(q, dx))

    def spread(q):
        for dy in (2, 1, 3, 0):
            for h in range(2):
                copies = first_stage(q, dy, h)
                if dy == 0:
                    start(copies)
                else:
                    copies[1]().start()

    def forward(q):
        for col in range(NY):
            for half in range(2):
                landed(b1.at[q, col, half], s1r.at[q, col, half])
        b2[q, x] = b1[q, x]
        for dx in (2, 1, 3):
            second_stage(q, dx).start()

    def deliver(q):
        for dx in (0, 2, 1, 3):
            if dx > 0:
                second_stage(q, dx).wait_recv()
            start(third_stage(q, dx))

    def finish(q, last):
        for col in range(NY):
            landed(fl.at[q, col], s3r.at[q, col])
        update(q, last)

    def compute(q):
        blocks = received[q]

        def per_row(i, carry):
            total = jnp.zeros((256, 256), jnp.float32)
            for m in range(NNB):
                total += jnp.dot(
                    w_v[i, m], blocks[slot[i * NNB + m]], preferred_element_type=jnp.float32
                )
            cs[q, i % 4, i // 4] = total.astype(jnp.bfloat16)
            return carry

        lax.fori_loop(0, ROWS, per_row, 0)

    def update(q, last):
        def per_pair(col, half, carry):
            row = 4 * half + q
            flipped = lax.dot_general(
                eye[...], fl[q, col, half], (((1,), (1,)), ((), ())),
                preferred_element_type=jnp.float32,
            )
            total = (
                k_v[row, col].astype(jnp.float32) + cs[col, q, half].astype(jnp.float32) + flipped
            )
            value = total / (vir[...] - occ[ig * ROWS + row] - occ[jg * CHUNKS + col])
            if last:
                stage[q, half, col] = value
            else:
                t_v[col][row] = value.astype(jnp.bfloat16)
            return carry

        for col in range(CHUNKS):
            lax.fori_loop(0, 2, functools.partial(per_pair, col), 0)
        if last:
            for half in range(2):
                out_copy(q, half).start()

    def out_copy(q, half):
        return pltpu.make_async_copy(
            stage.at[q, half], out_h.at[4 * half + q], out_sem.at[q, half]
        )

    def release(index, devices):
        for device in devices:
            pl.semaphore_signal(free.at[index], inc=1, device_id=device, device_id_type=MESH)

    x_peers = [(lax.rem(x + dx, NX) * NC + c, jg) for dx in range(1, NX)]
    y_peers = [(ig, lax.rem(y + dy, NY) * NZ + z) for dy in range(1, NY)]
    ring_peers = [(peer(dx, dc), jg) for dx, dc in ORDER]

    rows_of = lax.broadcasted_iota(jnp.int32, (256, 256), 0)
    cols_of = lax.broadcasted_iota(jnp.int32, (256, 256), 1)
    eye[...] = jnp.where(rows_of == cols_of, 1.0, 0.0).astype(jnp.bfloat16)
    across = jnp.broadcast_to(eps[...], (256, 256))
    vir[...] = across + across.T
    lax.fori_loop(0, NX * NC, choose, 0)
    lax.fori_loop(0, ROWS * NNB, locate, 0)
    for q in range(CHUNKS):
        t_load[q].wait()
        pack(q)
    pl.semaphore_wait(barrier, 18 - inside.astype(jnp.int32))

    for step in range(ITERS):
        first, last = step == 0, step == ITERS - 1
        if not first:
            for q in range(CHUNKS):
                for copy in exchange(q):
                    copy.wait_send()
            pl.semaphore_wait(free.at[0], len(ORDER))
            pack(0)
        for q in range(CHUNKS - 1):
            if not first:
                pack(q + 1)
            for copy in exchange(q):
                copy.start()
        if first:
            w_load.start()
            k_load.start()
            w_load.wait()
        else:
            for q in range(CHUNKS):
                settle(q)
            release(2, x_peers)
            release(3, y_peers)
            for dy in range(NY):
                for h in range(2):
                    meet(dy, h, free.at[1])
        for q in range(CHUNKS):
            for copy in exchange(q):
                copy.wait_recv()
            compute(q)
            if not first and q == 0:
                pl.semaphore_wait(free.at[1], 8 - inside.astype(jnp.int32))
            spread(q)
            if q >= 1:
                if not first and q == 1:
                    pl.semaphore_wait(free.at[2], NX - 1)
                forward(q - 1)
            if q == 1:
                for copy in exchange(CHUNKS - 1):
                    copy.start()
            if q == 2:
                if first:
                    k_load.wait()
                else:
                    pl.semaphore_wait(free.at[3], NY - 1)
                deliver(0)
        if not last:
            release(0, ring_peers)
        deliver(1)
        finish(0, last)
        forward(3)
        deliver(2)
        finish(1, last)
        deliver(3)
        finish(2, last)
        finish(3, last)

    for q in range(CHUNKS):
        for copy in exchange(q):
            copy.wait_send()
        settle(q)
        for half in range(2):
            out_copy(q, half).wait()


def body(t_start, integrals, weights, neighbours, eps_occ, eps_vir):
    block = (256, 256)
    bf16 = jnp.bfloat16
    smem = pl.BlockSpec(memory_space=pltpu.SMEM)
    anywhere = pl.BlockSpec(memory_space=pl.ANY)
    dma = pltpu.SemaphoreType.DMA
    listed = neighbours.T
    bits = jnp.where(
        (listed // ROWS)[:, :, None] == jnp.arange(NX * NC, dtype=jnp.int32),
        lax.shift_left(jnp.int32(1), listed % ROWS)[:, :, None],
        0,
    ).reshape(NNB, NX * NC, ROWS, NX * NC)
    masks = lax.reduce(bits, jnp.int32(0), lax.bitwise_or, (0, 2))
    return pl.pallas_call(
        sweeps_kernel,
        out_shape=jax.ShapeDtypeStruct((ROWS, CHUNKS) + block, jnp.float32),
        in_specs=[smem] * 3 + [pl.BlockSpec(memory_space=pltpu.VMEM)] + [anywhere] * 3,
        out_specs=anywhere,
        scratch_shapes=[pltpu.VMEM((ROWS,) + block, bf16)] * CHUNKS
        + [
            pltpu.VMEM((ROWS, CHUNKS) + block, bf16),
            pltpu.VMEM((ROWS, NNB) + block, bf16),
            pltpu.VMEM((CHUNKS, NX * NC * CAP) + block, bf16),
        ]
        + [pltpu.VMEM((NX * NC * CAP,) + block, bf16)] * CHUNKS
        + [pltpu.VMEM((CHUNKS, 4, 2) + block, bf16)] * 4
        + [
            pltpu.VMEM(block, bf16),
            pltpu.VMEM(block, jnp.float32),
            pltpu.VMEM((CHUNKS, 2, 4) + block, jnp.float32),
            pltpu.SMEM((NX * NC * CAP,), jnp.int32),
            pltpu.SMEM((ROWS * NNB,), jnp.int32),
            dma((CHUNKS + 2,)),
            dma((CHUNKS, 8)),
            dma((CHUNKS, 8)),
            dma((CHUNKS, 4, 2)),
            dma((CHUNKS, 4, 2)),
            dma((CHUNKS, 4)),
            dma((CHUNKS, 4)),
            dma((CHUNKS, 4)),
            dma((CHUNKS, 4)),
            dma((CHUNKS, 2)),
            pltpu.SemaphoreType.REGULAR((4,)),
        ],
        compiler_params=pltpu.CompilerParams(
            collective_id=0, has_side_effects=True, vmem_limit_bytes=67043328
        ),
        name="sweeps",
    )(masks, listed, eps_occ, eps_vir.reshape(1, 256), t_start, integrals, weights)


def solution(mesh):
    placed = (
        P("igrp", "jgrp", None, None),
        P("igrp", "jgrp", None, None),
        P("igrp", None, None, None),
        P(),
        P(),
        P(),
    )
    return jax.shard_map(
        body, mesh=mesh, in_specs=placed, out_specs=P("igrp", "jgrp", None, None), check_vma=False
    )
```

```python
import functools

import jax
import jax.numpy as jnp
from jax import lax
from jax.experimental import pallas as pl
from jax.experimental.pallas import tpu as pltpu
from jax.sharding import PartitionSpec as P

NNB = 8
CAP = 2
ITERS = 2
MESH = pl.DeviceIdType.MESH
NX, NC, NY, NZ = 4, 2, 4, 4
COLS = 4
ROWS = 8
CHUNKS = ((0, 0, 256), (1, 0, 256), (2, 0, 256), (3, 0, 128), (3, 128, 128))
COUNT = len(CHUNKS)
WHOLE = 3
SCHEDULE = (
    "E0", "E1", "E2", "C0", "C1", "F0", "E3", "E4", "C2", "F1", "D0", "C3",
    "F2", "C4", "F3", "D1", "U0", "F4", "D2", "U1", "D3", "U2", "D4", "U3",
    "U4",
)
SPREAD = (2, 1, 3, 0)
ORDER = ((2, 0), (1, 0), (3, 0), (2, 1), (1, 1), (3, 1), (0, 1))


def sweeps_kernel(
    masks, listed, occ, eps, t_h, k_h, w_h, out_v,
    t_0, t_1, t_2, t_3, k_v, w_v, r_0, r_1, r_2, r_3, r_4,
    pk_w, cs_w, b1_w, b2_w, fl_w, pk_p, cs_p, b1_p, b2_p, fl_p, eye, vir,
    choice, slot, load_sem, es, er, s1s, s1r, s2s, s2r, s3s, s3r, free,
):
    ig = lax.axis_index("igrp")
    jg = lax.axis_index("jgrp")
    x, c = ig // NC, ig % NC
    y, z = jg // NZ, jg % NZ
    received = (r_0, r_1, r_2, r_3, r_4)

    def of(whole, part):
        return [whole.at[q] if q < WHOLE else part.at[q - WHOLE] for q in range(COUNT)]

    pk, cs, b1 = of(pk_w, pk_p), of(cs_w, cs_p), of(b1_w, b1_p)
    b2, fl = of(b2_w, b2_p), of(fl_w, fl_p)
    t_v = (t_0, t_1, t_2, t_3)

    def peer(dx, dc):
        return lax.rem(x + dx, NX) * NC + lax.rem(c + dc, NC)

    t_load = [
        pltpu.make_async_copy(t_h.at[:, q], t_v[q], load_sem.at[q]) for q in range(COLS)
    ]
    w_load = pltpu.make_async_copy(w_h, w_v, load_sem.at[COLS])
    k_load = pltpu.make_async_copy(k_h, k_v, load_sem.at[COLS + 1])
    for load in t_load:
        load.start()

    barrier = pltpu.get_barrier_semaphore()
    inside = z // 2 == c
    for dx, dc in ORDER:
        pl.semaphore_signal(barrier, inc=1, device_id=(peer(dx, dc), jg), device_id_type=MESH)
    for dy in range(1, NY):
        pl.semaphore_signal(
            barrier, inc=1, device_id=(ig, lax.rem(y + dy, NY) * NZ + z), device_id_type=MESH
        )
    def meet(dy, h, sem):
        def greet():
            pl.semaphore_signal(
                sem,
                inc=1,
                device_id=(x * NC + z // 2, lax.rem(y + dy, NY) * NZ + 2 * c + h),
                device_id_type=MESH,
            )

        if dy == 0:
            pl.when(jnp.logical_not(inside & (z == 2 * c + h)))(greet)
        else:
            greet()

    for dy in range(NY):
        for h in range(2):
            meet(dy, h, barrier)

    def place(bit):
        found = jnp.int32(0)
        for k in range(1, ROWS):
            found += (bit >= (1 << k)).astype(jnp.int32)
        return found

    def choose(p, carry):
        mask = masks[p, ig]
        low = mask & (0 - mask)
        choice[p * CAP] = place(low)
        choice[p * CAP + 1] = place(mask - low)
        return carry

    def locate(n, carry):
        orbital = listed[n % NNB, ig * ROWS + n // NNB]
        block = orbital // ROWS
        below = masks[ig, block] % lax.shift_left(jnp.int32(1), orbital % ROWS)
        slot[n] = block * CAP + (below > 0).astype(jnp.int32)
        return carry

    def pack(q):
        col, lo, width = CHUNKS[q]

        def one(n, carry):
            kk = n // CAP
            s = n % CAP
            dest = peer(kk // NC, kk % NC)
            pk[q][n] = t_v[col][choice[dest * CAP + s], :, lo : lo + width]
            return carry

        lax.fori_loop(CAP, NX * NC * CAP, one, 0)
        for s in range(CAP):
            received[q][ig * CAP + s] = t_v[col][choice[ig * CAP + s], :, lo : lo + width]

    def exchange(q):
        copies = []
        for dx, dc in ORDER:
            kk = dx * NC + dc
            copies.append(
                pltpu.make_async_remote_copy(
                    src_ref=pk[q].at[pl.ds(kk * CAP, CAP)],
                    dst_ref=received[q].at[pl.ds(ig * CAP, CAP)],
                    send_sem=es.at[q, kk],
                    recv_sem=er.at[q, kk],
                    device_id=(peer(dx, dc), jg),
                    device_id_type=MESH,
                )
            )
        return copies

    def start(copies):
        own, remote, local = copies
        pl.when(jnp.logical_not(own))(lambda: remote().start())
        pl.when(own)(lambda: local().start())

    def sent(copies):
        own, remote, local = copies
        pl.when(jnp.logical_not(own))(lambda: remote().wait_send())

    def landed(block, sem):
        pltpu.make_async_copy(block, block, sem).wait()

    def first_stage(q, dy, h):
        to = lax.rem(y + dy, NY)
        own = inside & (z == 2 * c + h) if dy == 0 else None
        source, target, arrival = cs[q].at[to, h], b1[q].at[y, z % 2], s1r.at[q, y, z % 2]

        def remote():
            return pltpu.make_async_remote_copy(
                src_ref=source,
                dst_ref=target,
                send_sem=s1s.at[q, dy, h],
                recv_sem=arrival,
                device_id=(x * NC + z // 2, to * NZ + 2 * c + h),
                device_id_type=MESH,
            )

        return own, remote, lambda: pltpu.make_async_copy(source, target, arrival)

    def second_stage(q, dx):
        to = lax.rem(x + dx, NX)
        return pltpu.make_async_remote_copy(
            src_ref=b1[q].at[to],
            dst_ref=b2[q].at[x],
            send_sem=s2s.at[q, dx],
            recv_sem=s2r.at[q, dx],
            device_id=(to * NC + c, jg),
            device_id_type=MESH,
        )

    def third_stage(q, dx):
        to = lax.rem(x + NX - dx, NX)
        source, target, arrival = b2[q].at[to], fl[q].at[y], s3r.at[q, y]

        def remote():
            return pltpu.make_async_remote_copy(
                src_ref=source,
                dst_ref=target,
                send_sem=s3s.at[q, dx],
                recv_sem=arrival,
                device_id=(ig, to * NZ + z),
                device_id_type=MESH,
            )

        return to == y, remote, lambda: pltpu.make_async_copy(source, target, arrival)

    def settle(q):
        for dy in range(NY):
            for h in range(2):
                copies = first_stage(q, dy, h)
                if dy == 0:
                    sent(copies)
                else:
                    copies[1]().wait_send()
        for dx in range(1, NX):
            second_stage(q, dx).wait_send()
        for dx in range(NX):
            sent(third_stage(q, dx))

    def spread(q):
        for dy in SPREAD:
            for h in range(2):
                copies = first_stage(q, dy, h)
                if dy == 0:
                    start(copies)
                else:
                    copies[1]().start()

    def forward(q):
        for col in range(NY):
            for half in range(2):
                landed(b1[q].at[col, half], s1r.at[q, col, half])
        b2[q][x] = b1[q][x]
        for dx in (2, 1, 3):
            second_stage(q, dx).start()

    def deliver(q):
        for dx in (0, 2, 1, 3):
            if dx > 0:
                second_stage(q, dx).wait_recv()
            start(third_stage(q, dx))

    def finish(q, last):
        for col in range(NY):
            landed(fl[q].at[col], s3r.at[q, col])
        update(q, last)

    def compute(q):
        blocks = received[q]

        def per_row(i, carry):
            total = jnp.zeros((256, CHUNKS[q][2]), jnp.float32)
            for m in range(NNB):
                total += jnp.dot(
                    w_v[i, m], blocks[slot[i * NNB + m]], preferred_element_type=jnp.float32
                )
            cs[q][i % 4, i // 4] = total.astype(jnp.bfloat16)
            return carry

        lax.fori_loop(0, ROWS, per_row, 0)

    def update(q, last):
        line, lo, width = CHUNKS[q]
        part = slice(lo, lo + width)

        def per_pair(col, half, carry):
            row = 4 * half + line
            flipped = lax.dot_general(
                eye[:width, :width], fl[q][col, half], (((1,), (1,)), ((), ())),
                preferred_element_type=jnp.float32,
            )
            if col < WHOLE:
                own = cs[col][line, half, part, :]
            else:
                own = jnp.concatenate(
                    [cs[k][line, half, part, :] for k in range(COUNT) if CHUNKS[k][0] == col],
                    axis=1,
                )
            total = (
                k_v[row, col, part, :].astype(jnp.float32) + own.astype(jnp.float32) + flipped
            )
            value = total / (vir[part, :] - occ[ig * ROWS + row] - occ[jg * COLS + col])
            if last:
                out_v[row, col, part, :] = value
            else:
                t_v[col][row, part, :] = value.astype(jnp.bfloat16)
            return carry

        for col in range(COLS):
            lax.fori_loop(0, 2, functools.partial(per_pair, col), 0)

    def release(index, devices):
        for device in devices:
            pl.semaphore_signal(free.at[index], inc=1, device_id=device, device_id_type=MESH)

    x_peers = [(lax.rem(x + dx, NX) * NC + c, jg) for dx in range(1, NX)]
    y_peers = [(ig, lax.rem(y + dy, NY) * NZ + z) for dy in range(1, NY)]
    ring_peers = [(peer(dx, dc), jg) for dx, dc in ORDER]

    rows_of = lax.broadcasted_iota(jnp.int32, (256, 256), 0)
    cols_of = lax.broadcasted_iota(jnp.int32, (256, 256), 1)
    eye[...] = jnp.where(rows_of == cols_of, 1.0, 0.0).astype(jnp.bfloat16)
    across = jnp.broadcast_to(eps[...], (256, 256))
    vir[...] = across + across.T
    lax.fori_loop(0, NX * NC, choose, 0)
    lax.fori_loop(0, ROWS * NNB, locate, 0)
    for load in t_load:
        load.wait()
    for q in range(COUNT):
        pack(q)
    pl.semaphore_wait(barrier, 18 - inside.astype(jnp.int32))

    for step in range(ITERS):
        first, last = step == 0, step == ITERS - 1
        if not first:
            for q in range(COUNT):
                for copy in exchange(q):
                    copy.wait_send()
            pl.semaphore_wait(free.at[0], len(ORDER))
            pack(0)
        early = [name[0] for name in SCHEDULE].index("C")
        for q in range(early):
            if not first and q + 1 < COUNT:
                pack(q + 1)
            for copy in exchange(q):
                copy.start()
        if first:
            w_load.start()
            k_load.start()
            w_load.wait()
        else:
            for q in range(early + 1, COUNT):
                pack(q)
            for q in range(COUNT):
                settle(q)
            release(2, x_peers)
            release(3, y_peers)
            for dy in range(NY):
                for h in range(2):
                    meet(dy, h, free.at[1])
        waiting = {"S", "F", "D", "U"}
        for name in SCHEDULE[early:]:
            kind, q = name[0], int(name[1:])
            if kind == "E":
                for copy in exchange(q):
                    copy.start()
            elif kind == "C":
                for copy in exchange(q):
                    copy.wait_recv()
                compute(q)
                if not first and "S" in waiting:
                    pl.semaphore_wait(free.at[1], 8 - inside.astype(jnp.int32))
                waiting.discard("S")
                spread(q)
                if not last and q == COUNT - 1:
                    release(0, ring_peers)
            elif kind == "F":
                if not first and "F" in waiting:
                    pl.semaphore_wait(free.at[2], NX - 1)
                waiting.discard("F")
                forward(q)
            elif kind == "D":
                if not first and "D" in waiting:
                    pl.semaphore_wait(free.at[3], NY - 1)
                waiting.discard("D")
                deliver(q)
            else:
                if first and "U" in waiting:
                    k_load.wait()
                waiting.discard("U")
                finish(q, last)

    for q in range(COUNT):
        for copy in exchange(q):
            copy.wait_send()
        settle(q)


def body(t_start, integrals, weights, neighbours, eps_occ, eps_vir):
    block = (256, 256)
    bf16 = jnp.bfloat16
    smem = pl.BlockSpec(memory_space=pltpu.SMEM)
    anywhere = pl.BlockSpec(memory_space=pl.ANY)
    dma = pltpu.SemaphoreType.DMA

    def relayed(number, width):
        sent = pltpu.VMEM((number, NX * NC * CAP, 256, width), bf16)
        return [sent] + [pltpu.VMEM((number, 4, 2, 256, width), bf16)] * 4

    listed = neighbours.T
    bits = jnp.where(
        (listed // ROWS)[:, :, None] == jnp.arange(NX * NC, dtype=jnp.int32),
        lax.shift_left(jnp.int32(1), listed % ROWS)[:, :, None],
        0,
    ).reshape(NNB, NX * NC, ROWS, NX * NC)
    masks = lax.reduce(bits, jnp.int32(0), lax.bitwise_or, (0, 2))
    return pl.pallas_call(
        sweeps_kernel,
        out_shape=pltpu.VMEM((ROWS, COLS) + block, jnp.float32),
        in_specs=[smem] * 3 + [pl.BlockSpec(memory_space=pltpu.VMEM)] + [anywhere] * 3,
        out_specs=pl.BlockSpec(memory_space=pltpu.VMEM),
        scratch_shapes=[pltpu.VMEM((ROWS,) + block, bf16)] * COLS
        + [pltpu.VMEM((ROWS, COLS) + block, bf16), pltpu.VMEM((ROWS, NNB) + block, bf16)]
        + [pltpu.VMEM((NX * NC * CAP, 256, width), bf16) for _, _, width in CHUNKS]
        + relayed(WHOLE, 256)
        + relayed(COUNT - WHOLE, 128)
        + [
            pltpu.VMEM(block, bf16),
            pltpu.VMEM(block, jnp.float32),
            pltpu.SMEM((NX * NC * CAP,), jnp.int32),
            pltpu.SMEM((ROWS * NNB,), jnp.int32),
            dma((COLS + 2,)),
            dma((COUNT, 8)),
            dma((COUNT, 8)),
            dma((COUNT, 4, 2)),
            dma((COUNT, 4, 2)),
            dma((COUNT, 4)),
            dma((COUNT, 4)),
            dma((COUNT, 4)),
            dma((COUNT, 4)),
            pltpu.SemaphoreType.REGULAR((4,)),
        ],
        compiler_params=pltpu.CompilerParams(
            collective_id=0, has_side_effects=True, vmem_limit_bytes=52 * 2**20
        ),
        name="sweeps",
    )(masks, listed, eps_occ, eps_vir.reshape(1, 256), t_start, integrals, weights)


def solution(mesh):
    placed = (
        P("igrp", "jgrp", None, None),
        P("igrp", "jgrp", None, None),
        P("igrp", None, None, None),
        P(),
        P(),
        P(),
    )
    return jax.shard_map(
        body, mesh=mesh, in_specs=placed, out_specs=P("igrp", "jgrp", None, None), check_vma=False
    )
```
